32 devices in a mesh: groups: 2 (over y), wide: 4 (over z), narrow: 4 (over x, core).
Axes of the slice: x: 2, y: 2, z: 4, core: 2. Of those that a mesh axis runs over, the one named last changes fastest.
Arguments:
- hidden: bfloat16 [32, 8192], P('groups', 'wide'), parts along dimension 0, may hold values from -6 to 6
- w_query: bfloat16 [8192, 8192], P('wide', 'narrow'), may hold values from -0.0625 to 0.0625
- w_key: bfloat16 [8192, 1024], P('wide', 'narrow'), may hold values from -0.0625 to 0.0625
- w_value: bfloat16 [8192, 1024], P('wide', 'narrow'), may hold values from -0.0625 to 0.0625
- w_out: bfloat16 [8192, 8192], P('narrow', 'wide'), may hold values from -0.0625 to 0.0625
- key_cache: bfloat16 [32, 768, 8, 128], P(('groups', 'wide'), None, 'narrow'), parts along dimension 0, may hold values from -720 to 720
- value_cache: bfloat16 [32, 768, 8, 128], P(('groups', 'wide'), None, 'narrow'), parts along dimension 0, may hold values from -6 to 6
- cycle_offset: int32 [32], P(('groups', 'wide')), parts along dimension 0, may hold values from 0 to 767
- valid_length: int32 [32], P(('groups', 'wide')), parts along dimension 0, may hold values from 1 to 768, as said below
- slot_of: int32 [32], P('groups'), parts along dimension 0, may hold values from 0 to 15, as said below
Outputs:
- attn_out: bfloat16 [32, 8192], P('groups', 'wide'), parts along dimension 0
- new_keys: bfloat16 [32, 1024], P(('groups', 'wide'), 'narrow'), parts along dimension 0
- new_values: bfloat16 [32, 1024], P(('groups', 'wide'), 'narrow'), parts along dimension 0
The draws below stay inside these ranges and needn't reach their ends.
There are 2 independent parts, one for each index of `groups`. The reference program is written for one: setup_inputs(seed, part) draws one part's arguments, and reference() takes and returns one part's arrays. A program takes and returns all parts, laid end to end along the dimension named above; an argument that names none is the same for every part. Nothing has to cross between parts.
Inputs may be any that keep to these rules, and one draw needn't show every extreme that they name: Requests are in 4 microbatches of consecutive rows; each cache owner (a block of 4 consecutive slots) holds exactly 1 request of each microbatch m, at the slots owner * 4 + m + j for 0 <= j < 1; slot_of is a permutation. `valid_length`: at least one slot has a full cycle.
All inputs are finite; a program needn't handle non-finite values.
Results may differ from the reference program's by a relative error of at most 0.012.
Values may be sent and summed in bfloat16 or wider, within the bound.
A program may use at most 64 MiB of HBM per device.

```python
import jax
import jax.numpy as jnp
from jax import lax

D = 8192
HQ = 64
KV = 8
HD = 128
L = 768
SLOT_MB = 1
MICRO = 4
REQ_DEV = 4
REQUESTS = 16


def draw_key_cache(key, part):
    base = jax.random.normal(jax.random.fold_in(key, 11), (REQUESTS, L, KV, HD), jnp.float32)
    base = jnp.clip(base, -6.0, 6.0)
    return base.astype(jnp.bfloat16)


def draw_valid_length(key, part):
    lengths = jax.random.randint(jax.random.fold_in(key, 21), (REQUESTS,), 1, L + 1)
    longest = jax.random.randint(jax.random.fold_in(key, 22), (), 0, REQUESTS)
    return jnp.where(jnp.arange(REQUESTS, dtype=jnp.int32) == longest, L, lengths).astype(jnp.int32)


def draw_slot_of(key, part):
    rows_block = REQUESTS // MICRO
    block_keys = jax.random.split(jax.random.fold_in(key, 31), MICRO)

    def shuffle(one_key):
        return jax.random.permutation(one_key, rows_block)
    perms = jax.vmap(shuffle)(block_keys)
    blocks = jnp.arange(MICRO, dtype=jnp.int32)[:, None]
    owner = perms // SLOT_MB
    within = perms % SLOT_MB
    slots = owner * REQ_DEV + blocks * SLOT_MB + within
    return slots.reshape(REQUESTS).astype(jnp.int32)


def touch_ends(result, stream_key, least, top_value):
    shape = result.shape
    spot = [jax.random.randint(jax.random.fold_in(stream_key, axis), (), 0, shape[axis]) for axis in range(len(shape))]
    result = result.at[tuple(spot)].set(least)
    longest = shape.index(max(shape))
    spot[longest] = (spot[longest] + 1) % shape[longest]
    return result.at[tuple(spot)].set(top_value)


def level_of(stream_key, extent, pieces, least, high):
    def one(position, parts):
        heights = jax.random.uniform(jax.random.fold_in(jax.random.fold_in(stream_key, 6), position), (parts,), jnp.float32, least / len(pieces), high / len(pieces))
        return jnp.repeat(jnp.exp(heights), extent[position] // parts).reshape((-1,) + (1,) * (len(extent) - position - 1))

    gain = one(*pieces[0])
    for cut in pieces[1:]:
        gain = gain * one(*cut)
    return gain


def gaussian(own_key, shape, width, bound, pieces=(), kind=jnp.bfloat16):
    factor_of = level_of(own_key, shape, pieces, -0.22, 0.18) if pieces else 1.0
    values = jax.random.normal(own_key, shape, jnp.float32) * width * factor_of
    return jnp.minimum(jnp.maximum(values, -bound), bound).astype(kind)


def setup_inputs(seed: int = 0, part: int = 0) -> dict:
    splits = jax.random.split(jax.random.key(seed), 11)
    part_splits = jax.random.split(jax.random.fold_in(splits[10], part), 11)
    return {
        "hidden": gaussian(part_splits[0], (REQUESTS, D), 1.0, 6.0, ((1, 4),)),
        "w_query": gaussian(splits[1], (D, HQ * HD), D ** -0.5, 0.0625, ((0, 4), (1, 4))),
        "w_key": gaussian(splits[2], (D, KV * HD), D ** -0.5, 0.0625, ((0, 4), (1, 4))),
        "w_value": gaussian(splits[3], (D, KV * HD), D ** -0.5, 0.0625, ((0, 4), (1, 4))),
        "w_out": gaussian(splits[4], (HQ * HD, D), (HQ * HD) ** -0.5, 0.0625, ((0, 4), (1, 4))),
        "key_cache": draw_key_cache(jax.random.fold_in(jax.random.fold_in(splits[10], part), 71), part),
        "value_cache": gaussian(part_splits[6], (REQUESTS, L, KV, HD), 1.0, 6.0, ((0, 4), (2, 4))),
        "cycle_offset": touch_ends(jax.random.randint(part_splits[7], (REQUESTS,), 0, L), jax.random.fold_in(part_splits[7], 1), 0, L - 1).astype(jnp.int32),
        "valid_length": draw_valid_length(jax.random.fold_in(jax.random.fold_in(splits[10], part), 71), part),
        "slot_of": draw_slot_of(jax.random.fold_in(jax.random.fold_in(splits[10], part), 71), part),
    }


def reference(hidden, w_query, w_key, w_value, w_out, key_cache, value_cache, cycle_offset, valid_length, slot_of):
    order = jnp.zeros((REQUESTS,), jnp.int32).at[slot_of].set(jnp.arange(REQUESTS, dtype=jnp.int32))
    slot_rows = hidden[order]
    queries = jnp.dot(slot_rows, w_query, preferred_element_type=jnp.float32).astype(jnp.bfloat16)
    new_keys = jnp.dot(slot_rows, w_key, preferred_element_type=jnp.float32).astype(jnp.bfloat16)
    new_values = jnp.dot(slot_rows, w_value, preferred_element_type=jnp.float32).astype(jnp.bfloat16)
    group = HQ // KV
    scale = 1.0 / jnp.sqrt(jnp.float32(HD))

    def one_slot(items):
        query_row, key_row, value_row, keys_old, values_old, offset, length = items
        keys_all = keys_old.at[offset].set(key_row.reshape(KV, HD))
        values_all = values_old.at[offset].set(value_row.reshape(KV, HD))
        query_heads = query_row.reshape(KV, group, HD).astype(jnp.float32)
        scores = jnp.einsum('kgd,jkd->kgj', query_heads, keys_all.astype(jnp.float32)) * scale
        distance = (offset - jnp.arange(L, dtype=jnp.int32)) % L
        usable = (distance < length)[None, None, :]
        masked = jnp.where(usable, scores, -jnp.inf)
        top = lax.optimization_barrier(jnp.max(masked, axis=2, keepdims=True))
        spread = jnp.where(usable, jnp.exp(masked - top), 0.0)
        probs = (spread / lax.optimization_barrier(jnp.sum(spread, axis=2, keepdims=True))).astype(jnp.bfloat16)
        mixed = jnp.einsum('kgj,jkd->kgd', probs.astype(jnp.float32), values_all.astype(jnp.float32))
        return mixed.astype(jnp.bfloat16).reshape(HQ * HD)
    heads = lax.map(one_slot, (queries, new_keys, new_values, key_cache, value_cache, cycle_offset, valid_length))
    projected = jnp.dot(heads, w_out, preferred_element_type=jnp.float32)
    attn_out = projected[slot_of].astype(jnp.bfloat16)
    return (attn_out, new_keys, new_values)
```

```python
import functools

import jax
import jax.numpy as jnp
from jax import lax
from jax.experimental import pallas as pl
from jax.experimental.pallas import tpu as pltpu
from jax.sharding import PartitionSpec as P

masked_low = -1e30
MESH = pl.DeviceIdType.MESH


def width_of(columns, most):
    width = min(columns, most)
    while columns % width:
        width -= 128
    return width


def kernel(
    wide,
    narrow,
    kv_local,
    q_width,
    o_width,
    hidden,
    w_query,
    w_key,
    w_value,
    w_out,
    key_cache,
    value_cache,
    slot_row,
    cycle_offset,
    valid_length,
    attn_out,
    new_keys,
    new_values,
    wq,
    wk,
    wv,
    wo,
    keys,
    values,
    part,
    got,
    query_heads,
    mixed_heads,
    heads_own,
    heads_got,
    heads_full,
    out_part,
    out_got,
    in_sem,
    send_sem,
    recv_sem,
    head_send,
    head_recv,
    out_send,
    out_recv,
):
    me_wide = lax.axis_index("wide")
    me_narrow = lax.axis_index("narrow")
    requests = hidden.shape[0]
    slots = keys.shape[0]
    head_dim = keys.shape[2]
    span = keys.shape[1]
    window = span // kv_local
    query_cols = wq.shape[1]
    key_cols = wk.shape[1]
    out_cols = wo.shape[1]
    heads_local = query_cols // head_dim
    group = heads_local // kv_local
    q_chunks = query_cols // q_width
    o_chunks = out_cols // o_width

    first = [
        pltpu.make_async_copy(w_key, wk, in_sem.at[0]),
        pltpu.make_async_copy(w_value, wv, in_sem.at[1]),
    ]
    for c in range(q_chunks):
        cols = pl.ds(c * q_width, q_width)
        first.append(pltpu.make_async_copy(w_query.at[:, cols], wq.at[:, cols], in_sem.at[2 + c]))
    base = 2 + q_chunks
    cache_in = [
        pltpu.make_async_copy(key_cache, keys, in_sem.at[base]),
        pltpu.make_async_copy(value_cache, values, in_sem.at[base + 1]),
    ]
    out_in = []
    for c in range(o_chunks):
        cols = pl.ds(c * o_width, o_width)
        out_in.append(
            pltpu.make_async_copy(w_out.at[:, cols], wo.at[:, cols], in_sem.at[base + 2 + c])
        )
    for copy in first:
        copy.start()

    barrier = pltpu.get_barrier_semaphore()
    for d in range(1, wide):
        pl.semaphore_signal(
            barrier,
            inc=1,
            device_id={"wide": lax.rem(me_wide + d, wide)},
            device_id_type=MESH,
        )
    for d in range(1, narrow):
        pl.semaphore_signal(
            barrier,
            inc=1,
            device_id={"narrow": lax.rem(me_narrow + d, narrow)},
            device_id_type=MESH,
        )

    slot_id = lax.broadcasted_iota(jnp.int32, (requests, requests), 0)
    pick = jnp.where(slot_row[...] == slot_id, 1.0, 0.0)
    rows = jnp.dot(
        pick.astype(jnp.bfloat16), hidden[...], preferred_element_type=jnp.float32
    ).astype(jnp.bfloat16)

    def to_owner(block, d, col, width):
        peer = lax.rem(me_wide + d, wide)
        return pltpu.make_async_remote_copy(
            src_ref=part.at[peer, :, pl.ds(col, width)],
            dst_ref=got.at[d, :, pl.ds(col, width)],
            send_sem=send_sem.at[block, d],
            recv_sem=recv_sem.at[block, d],
            device_id={"wide": peer},
            device_id_type=MESH,
        )

    blocks = [(query_cols, 2 * key_cols)] + [(c * q_width, q_width) for c in range(q_chunks)]
    for block, (col, width) in enumerate(blocks):
        if block == 0:
            first[0].wait()
            sums = jnp.dot(rows, wk[...], preferred_element_type=jnp.float32)
            for w in range(wide):
                part[w, :, col : col + key_cols] = sums[w * slots : (w + 1) * slots]
            first[1].wait()
            sums = jnp.dot(rows, wv[...], preferred_element_type=jnp.float32)
            for w in range(wide):
                part[w, :, col + key_cols : col + width] = sums[w * slots : (w + 1) * slots]
            pl.semaphore_wait(barrier, wide + narrow - 2)
        else:
            first[1 + block].wait()
            sums = jnp.dot(rows, wq[:, col : col + width], preferred_element_type=jnp.float32)
            for w in range(wide):
                part[w, :, col : col + width] = sums[w * slots : (w + 1) * slots]
        for d in range(1, wide):
            to_owner(block, d, col, width).start()
    for copy in cache_in + out_in:
        copy.start()

    place = lax.broadcasted_iota(jnp.int32, (1, span), 1)
    position = place // kv_local
    kv_of = place - position * kv_local
    row_kv = lax.broadcasted_iota(jnp.int32, (heads_local, 1), 0) // group
    same_head = row_kv == kv_of
    scale = 1.0 / jnp.sqrt(jnp.float32(head_dim))

    def summed(col, width):
        total = part[me_wide, :, col : col + width]
        for d in range(1, wide):
            total = total + got[d, :, col : col + width]
        return total

    for d in range(1, wide):
        to_owner(0, d, *blocks[0]).wait_recv()
    keys_new = summed(query_cols, key_cols).astype(jnp.bfloat16)
    values_new = summed(query_cols + key_cols, key_cols).astype(jnp.bfloat16)
    new_keys[...] = keys_new
    new_values[...] = values_new
    keys_fresh = keys_new.astype(jnp.float32)
    values_fresh = values_new.astype(jnp.float32)
    for block in range(1, len(blocks)):
        col, width = blocks[block]
        for d in range(1, wide):
            to_owner(block, d, col, width).wait_recv()
        for h in range(col // head_dim, (col + width) // head_dim):
            query_heads[:, h, :] = summed(h * head_dim, head_dim)

    for copy in cache_in:
        copy.wait()

    def by_head(fresh, s):
        result = jnp.broadcast_to(fresh[s : s + 1, :head_dim], (heads_local, head_dim))
        for k in range(1, kv_local):
            other = fresh[s : s + 1, k * head_dim : (k + 1) * head_dim]
            result = jnp.where(row_kv == k, other, result)
        return result

    for s in range(slots):
        query = query_heads[s].astype(jnp.bfloat16)
        scores = (
            lax.dot_general(
                query, keys[s], (((1,), (1,)), ((), ())), preferred_element_type=jnp.float32
            )
            * scale
        )
        own_score = (
            jnp.sum(query.astype(jnp.float32) * by_head(keys_fresh, s), axis=1, keepdims=True)
            * scale
        )
        offset = cycle_offset[s]
        distance = offset - position
        distance = jnp.where(distance < 0, distance + window, distance)
        usable = (distance > 0) & (distance < valid_length[s])
        masked = jnp.where(usable & same_head, scores, masked_low)
        top = jnp.maximum(jnp.max(masked, axis=1, keepdims=True), own_score)
        spread = jnp.exp(masked - top)
        own = jnp.exp(own_score - top)
        inverse = 1.0 / (jnp.sum(spread, axis=1, keepdims=True) + own)
        mixed = jnp.dot(
            (spread * inverse).astype(jnp.bfloat16), values[s], preferred_element_type=jnp.float32
        )
        own_weight = (own * inverse).astype(jnp.bfloat16).astype(jnp.float32)
        mixed_heads[s] = mixed + own_weight * by_head(values_fresh, s)

    for h in range(heads_local):
        heads_own[:, h * head_dim : (h + 1) * head_dim] = mixed_heads[:, h, :].astype(jnp.bfloat16)

    def to_wide(d):
        return pltpu.make_async_remote_copy(
            src_ref=heads_own,
            dst_ref=heads_got.at[d],
            send_sem=head_send.at[d],
            recv_sem=head_recv.at[d],
            device_id={"wide": lax.rem(me_wide + d, wide)},
            device_id_type=MESH,
        )

    for d in range(1, wide):
        to_wide(d).start()
    heads_full[0:slots] = heads_own[...].astype(jnp.float32)
    for d in range(1, wide):
        to_wide(d).wait_recv()
        heads_full[d * slots : (d + 1) * slots] = heads_got[d].astype(jnp.float32)
    held_row = lax.broadcasted_iota(jnp.int32, (requests, requests), 0)
    back = held_row // slots
    held_slot = lax.rem(me_wide - back + wide, wide) * slots + (held_row - back * slots)
    give = jnp.where(slot_row[...] == held_slot, 1.0, 0.0).astype(jnp.bfloat16)
    heads = lax.dot_general(
        give,
        heads_full[...].astype(jnp.bfloat16),
        (((0,), (0,)), ((), ())),
        preferred_element_type=jnp.float32,
    ).astype(jnp.bfloat16)

    def to_narrow(c, d):
        return pltpu.make_async_remote_copy(
            src_ref=out_part.at[c],
            dst_ref=out_got.at[c, me_narrow],
            send_sem=out_send.at[c, d],
            recv_sem=out_recv.at[c, d],
            device_id={"narrow": lax.rem(me_narrow + d, narrow)},
            device_id_type=MESH,
        )

    for c in range(o_chunks):
        cols = slice(c * o_width, (c + 1) * o_width)
        out_in[c].wait()
        sums = jnp.dot(heads, wo[:, cols], preferred_element_type=jnp.float32)
        out_part[c] = sums.astype(jnp.bfloat16)
        for d in range(1, narrow):
            to_narrow(c, d).start()
        out_got[c, me_narrow] = sums.astype(jnp.bfloat16)
    for c in range(o_chunks):
        cols = slice(c * o_width, (c + 1) * o_width)
        for d in range(1, narrow):
            to_narrow(c, d).wait_recv()
        total = out_got[c, 0].astype(jnp.float32)
        for n in range(1, narrow):
            total = total + out_got[c, n].astype(jnp.float32)
        attn_out[:, cols] = total.astype(jnp.bfloat16)

    for block, (col, width) in enumerate(blocks):
        for d in range(1, wide):
            to_owner(block, d, col, width).wait_send()
    for d in range(1, wide):
        to_wide(d).wait_send()
    for c in range(o_chunks):
        for d in range(1, narrow):
            to_narrow(c, d).wait_send()


def per_device(
    wide,
    narrow,
    hidden,
    w_query,
    w_key,
    w_value,
    w_out,
    key_cache,
    value_cache,
    cycle_offset,
    valid_length,
    slot_of,
):
    requests = slot_of.shape[0]
    slots, window, kv_local, head_dim = key_cache.shape
    query_cols = w_query.shape[1]
    key_cols = w_key.shape[1]
    out_cols = w_out.shape[1]
    q_width = width_of(query_cols, 512)
    o_width = width_of(out_cols, 512)
    q_chunks = query_cols // q_width
    o_chunks = out_cols // o_width
    all_cols = query_cols + 2 * key_cols
    span = window * kv_local
    vmem = pl.BlockSpec(memory_space=pltpu.VMEM)
    smem = pl.BlockSpec(memory_space=pltpu.SMEM)
    anywhere = pl.BlockSpec(memory_space=pl.ANY)
    return pl.pallas_call(
        functools.partial(kernel, wide, narrow, kv_local, q_width, o_width),
        out_shape=(
            jax.ShapeDtypeStruct((requests, out_cols), jnp.bfloat16),
            jax.ShapeDtypeStruct((slots, key_cols), jnp.bfloat16),
            jax.ShapeDtypeStruct((slots, key_cols), jnp.bfloat16),
        ),
        in_specs=[vmem] + [anywhere] * 6 + [vmem, smem, smem],
        out_specs=(vmem, vmem, vmem),
        scratch_shapes=[
            pltpu.VMEM(w_query.shape, jnp.bfloat16),
            pltpu.VMEM(w_key.shape, jnp.bfloat16),
            pltpu.VMEM(w_value.shape, jnp.bfloat16),
            pltpu.VMEM(w_out.shape, jnp.bfloat16),
            pltpu.VMEM((slots, span, head_dim), jnp.bfloat16),
            pltpu.VMEM((slots, span, head_dim), jnp.bfloat16),
            pltpu.VMEM((wide, slots, all_cols), jnp.float32),
            pltpu.VMEM((wide, slots, all_cols), jnp.float32),
            pltpu.VMEM((slots, query_cols // head_dim, head_dim), jnp.float32),
            pltpu.VMEM((slots, query_cols // head_dim, head_dim), jnp.float32),
            pltpu.VMEM((slots, query_cols), jnp.bfloat16),
            pltpu.VMEM((wide, slots, query_cols), jnp.bfloat16),
            pltpu.VMEM((wide * slots, query_cols), jnp.float32),
            pltpu.VMEM((o_chunks, requests, o_width), jnp.bfloat16),
            pltpu.VMEM((o_chunks, narrow, requests, o_width), jnp.bfloat16),
            pltpu.SemaphoreType.DMA((4 + q_chunks + o_chunks,)),
            pltpu.SemaphoreType.DMA((1 + q_chunks, wide)),
            pltpu.SemaphoreType.DMA((1 + q_chunks, wide)),
            pltpu.SemaphoreType.DMA((wide,)),
            pltpu.SemaphoreType.DMA((wide,)),
            pltpu.SemaphoreType.DMA((o_chunks, narrow)),
            pltpu.SemaphoreType.DMA((o_chunks, narrow)),
        ],
        compiler_params=pltpu.CompilerParams(
            collective_id=0, has_side_effects=True, vmem_limit_bytes=60 * 1024 * 1024
        ),
        name="decode_step",
    )(
        hidden,
        w_query,
        w_key,
        w_value,
        w_out,
        key_cache.reshape(slots, span, head_dim),
        value_cache.reshape(slots, span, head_dim),
        slot_of.reshape(1, requests),
        cycle_offset,
        valid_length,
    )


def solution(mesh):
    placed = (
        P("groups", "wide"),
        P("wide", "narrow"),
        P("wide", "narrow"),
        P("wide", "narrow"),
        P("narrow", "wide"),
        P(("groups", "wide"), None, "narrow", None),
        P(("groups", "wide"), None, "narrow", None),
        P(("groups", "wide")),
        P(("groups", "wide")),
        P("groups"),
    )
    return jax.shard_map(
        functools.partial(per_device, mesh.shape["wide"], mesh.shape["narrow"]),
        mesh=mesh,
        in_specs=placed,
        out_specs=(
            P("groups", "wide"),
            P(("groups", "wide"), "narrow"),
            P(("groups", "wide"), "narrow"),
        ),
        check_vma=False,
    )
```

```python
import functools

import jax
import jax.numpy as jnp
from jax import lax
from jax.experimental import pallas as pl
from jax.experimental.pallas import tpu as pltpu
from jax.sharding import PartitionSpec as P

masked_low = -1e30
MESH = pl.DeviceIdType.MESH


def width_of(columns, most):
    width = min(columns, most)
    while columns % width:
        width -= 128
    return width


def kernel(
    wide,
    narrow,
    kv_local,
    q_width,
    o_width,
    hidden_in,
    w_query,
    w_key,
    w_value,
    w_out,
    key_cache,
    value_cache,
    slot_row_in,
    cycle_offset_in,
    valid_length_in,
    attn_out,
    new_keys,
    new_values,
    hidden,
    slot_row,
    cycle_offset,
    valid_length,
    wq,
    wk,
    wv,
    wo,
    keys,
    values,
    part,
    pair_got,
    pair_sum,
    got,
    query_heads,
    heads_own,
    heads_got,
    heads_full,
    out_part,
    out_got,
    in_sem,
    small_sem,
    pair_send,
    pair_recv,
    send_sem,
    recv_sem,
    head_send,
    head_recv,
    out_send,
    out_recv,
):
    me_wide = lax.axis_index("wide")
    me_narrow = lax.axis_index("narrow")
    pairs = wide // 2
    my_pair = me_wide // 2
    side = me_wide - 2 * my_pair
    requests = hidden.shape[0]
    slots = keys.shape[0]
    head_dim = keys.shape[2]
    span = keys.shape[1]
    window = span // kv_local
    query_cols = wq.shape[1]
    key_cols = wk.shape[1]
    out_cols = wo.shape[1]
    heads_local = query_cols // head_dim
    group = heads_local // kv_local
    q_chunks = query_cols // q_width
    o_chunks = out_cols // o_width

    first = [
        pltpu.make_async_copy(w_key, wk, in_sem.at[0]),
        pltpu.make_async_copy(w_value, wv, in_sem.at[1]),
    ]
    for c in range(q_chunks):
        cols = pl.ds(c * q_width, q_width)
        first.append(pltpu.make_async_copy(w_query.at[:, cols], wq.at[:, cols], in_sem.at[2 + c]))
    base = 2 + q_chunks
    cache_in = [
        pltpu.make_async_copy(key_cache, keys, in_sem.at[base]),
        pltpu.make_async_copy(value_cache, values, in_sem.at[base + 1]),
    ]
    out_in = []
    for c in range(o_chunks):
        cols = pl.ds(c * o_width, o_width)
        out_in.append(
            pltpu.make_async_copy(w_out.at[:, cols], wo.at[:, cols], in_sem.at[base + 2 + c])
        )
    small = [
        pltpu.make_async_copy(hidden_in, hidden, small_sem.at[0]),
        pltpu.make_async_copy(slot_row_in, slot_row, small_sem.at[1]),
        pltpu.make_async_copy(cycle_offset_in, cycle_offset, small_sem.at[2]),
        pltpu.make_async_copy(valid_length_in, valid_length, small_sem.at[3]),
    ]
    for copy in small + first:
        copy.start()

    barrier = pltpu.get_barrier_semaphore()
    peers = wide + narrow - 2
    for d in range(1, wide):
        pl.semaphore_signal(
            barrier,
            inc=1,
            device_id={"wide": lax.rem(me_wide + d, wide)},
            device_id_type=MESH,
        )
    for d in range(1, narrow):
        pl.semaphore_signal(
            barrier,
            inc=1,
            device_id={"narrow": lax.rem(me_narrow + d, narrow)},
            device_id_type=MESH,
        )

    small[0].wait()
    small[1].wait()
    slot_id = lax.broadcasted_iota(jnp.int32, (requests, requests), 0)
    pick = jnp.where(slot_row[...] == slot_id, 1.0, 0.0)
    rows = jnp.dot(
        pick.astype(jnp.bfloat16), hidden[...], preferred_element_type=jnp.float32
    ).astype(jnp.bfloat16)

    def to_neighbour(block, col, width):
        return pltpu.make_async_remote_copy(
            src_ref=part.at[1 - side, :, :, pl.ds(col, width)],
            dst_ref=pair_got.at[:, :, pl.ds(col, width)],
            send_sem=pair_send.at[block],
            recv_sem=pair_recv.at[block],
            device_id={"wide": 2 * my_pair + 1 - side},
            device_id_type=MESH,
        )

    def to_owner(block, d, col, width):
        other = lax.rem(my_pair + d, pairs)
        return pltpu.make_async_remote_copy(
            src_ref=pair_sum.at[other, :, pl.ds(col, width)],
            dst_ref=got.at[d, :, pl.ds(col, width)],
            send_sem=send_sem.at[block, d],
            recv_sem=recv_sem.at[block, d],
            device_id={"wide": 2 * other + side},
            device_id_type=MESH,
        )

    blocks = [(query_cols, 2 * key_cols)] + [(c * q_width, q_width) for c in range(q_chunks)]

    def keep(sums, col, width):
        for w in range(wide):
            part[w % 2, w // 2, :, col : col + width] = sums[w * slots : (w + 1) * slots]

    def join(block):
        col, width = blocks[block]
        to_neighbour(block, col, width).wait_recv()
        cols = slice(col, col + width)
        pair_sum[:, :, cols] = part[side, :, :, cols] + pair_got[:, :, cols]
        for d in range(1, pairs):
            to_owner(block, d, col, width).start()

    lag = 3
    for block, (col, width) in enumerate(blocks):
        if block == 0:
            first[0].wait()
            keep(jnp.dot(rows, wk[...], preferred_element_type=jnp.float32), col, key_cols)
            first[1].wait()
            keep(
                jnp.dot(rows, wv[...], preferred_element_type=jnp.float32),
                col + key_cols,
                key_cols,
            )
            pl.semaphore_wait(barrier, peers)
        else:
            first[1 + block].wait()
            keep(
                jnp.dot(rows, wq[:, col : col + width], preferred_element_type=jnp.float32),
                col,
                width,
            )
        to_neighbour(block, col, width).start()
        if block >= lag:
            join(block - lag)
    for copy in cache_in + out_in:
        copy.start()
    for block in range(max(len(blocks) - lag, 0), len(blocks)):
        join(block)

    place = lax.broadcasted_iota(jnp.int32, (1, span), 1)
    position = place // kv_local
    kv_of = place - position * kv_local
    row_kv = lax.broadcasted_iota(jnp.int32, (heads_local, 1), 0) // group
    same_head = row_kv == kv_of
    scale = 1.0 / jnp.sqrt(jnp.float32(head_dim))

    def summed(col, width):
        total = pair_sum[my_pair, :, col : col + width]
        for d in range(1, pairs):
            total = total + got[d, :, col : col + width]
        return total

    for d in range(1, pairs):
        to_owner(0, d, *blocks[0]).wait_recv()
    keys_new = summed(query_cols, key_cols).astype(jnp.bfloat16)
    values_new = summed(query_cols + key_cols, key_cols).astype(jnp.bfloat16)
    new_keys[...] = keys_new
    new_values[...] = values_new
    keys_fresh = keys_new.astype(jnp.float32)
    values_fresh = values_new.astype(jnp.float32)
    for block in range(1, len(blocks)):
        col, width = blocks[block]
        for d in range(1, pairs):
            to_owner(block, d, col, width).wait_recv()
        for h in range(col // head_dim, (col + width) // head_dim):
            query_heads[:, h, :] = summed(h * head_dim, head_dim)

    for copy in cache_in + small[2:]:
        copy.wait()

    def by_head(fresh, s):
        result = jnp.broadcast_to(fresh[s : s + 1, :head_dim], (heads_local, head_dim))
        for k in range(1, kv_local):
            other = fresh[s : s + 1, k * head_dim : (k + 1) * head_dim]
            result = jnp.where(row_kv == k, other, result)
        return result

    def to_wide(s, d):
        return pltpu.make_async_remote_copy(
            src_ref=heads_own.at[s],
            dst_ref=heads_got.at[d, s],
            send_sem=head_send.at[s, d],
            recv_sem=head_recv.at[s, d],
            device_id={"wide": lax.rem(me_wide + d, wide)},
            device_id_type=MESH,
        )

    for s in range(slots):
        query = query_heads[s].astype(jnp.bfloat16)
        scores = (
            lax.dot_general(
                query, keys[s], (((1,), (1,)), ((), ())), preferred_element_type=jnp.float32
            )
            * scale
        )
        own_score = (
            jnp.sum(query.astype(jnp.float32) * by_head(keys_fresh, s), axis=1, keepdims=True)
            * scale
        )
        offset = cycle_offset[s]
        distance = offset - position
        distance = jnp.where(distance < 0, distance + window, distance)
        usable = (distance > 0) & (distance < valid_length[s])
        masked = jnp.where(usable & same_head, scores, masked_low)
        top = jnp.maximum(jnp.max(masked, axis=1, keepdims=True), own_score)
        spread = jnp.exp(masked - top)
        own = jnp.exp(own_score - top)
        inverse = 1.0 / (jnp.sum(spread, axis=1, keepdims=True) + own)
        mixed = jnp.dot(
            (spread * inverse).astype(jnp.bfloat16), values[s], preferred_element_type=jnp.float32
        )
        own_weight = (own * inverse).astype(jnp.bfloat16).astype(jnp.float32)
        heads_own[s] = (mixed + own_weight * by_head(values_fresh, s)).astype(jnp.bfloat16)
        for d in range(1, wide):
            to_wide(s, d).start()

    heads_full[0:slots] = heads_own[...].astype(jnp.float32)
    for d in range(1, wide):
        for s in range(slots):
            to_wide(s, d).wait_recv()
        heads_full[d * slots : (d + 1) * slots] = heads_got[d].astype(jnp.float32)
    held_row = lax.broadcasted_iota(jnp.int32, (requests, requests), 0)
    back = held_row // slots
    held_slot = lax.rem(me_wide - back + wide, wide) * slots + (held_row - back * slots)
    give = jnp.where(slot_row[...] == held_slot, 1.0, 0.0).astype(jnp.bfloat16)
    by_slot = jnp.concatenate(
        [heads_full[:, h, :].astype(jnp.bfloat16) for h in range(heads_local)], axis=1
    )
    heads = lax.dot_general(
        give,
        by_slot,
        (((0,), (0,)), ((), ())),
        preferred_element_type=jnp.float32,
    ).astype(jnp.bfloat16)

    def to_narrow(c, d):
        return pltpu.make_async_remote_copy(
            src_ref=out_part.at[c],
            dst_ref=out_got.at[c, me_narrow],
            send_sem=out_send.at[c, d],
            recv_sem=out_recv.at[c, d],
            device_id={"narrow": lax.rem(me_narrow + d, narrow)},
            device_id_type=MESH,
        )

    for c in range(o_chunks):
        cols = slice(c * o_width, (c + 1) * o_width)
        out_in[c].wait()
        sums = jnp.dot(heads, wo[:, cols], preferred_element_type=jnp.float32)
        out_part[c] = sums.astype(jnp.bfloat16)
        for d in range(1, narrow):
            to_narrow(c, d).start()
        out_got[c, me_narrow] = sums.astype(jnp.bfloat16)
    for c in range(o_chunks):
        cols = slice(c * o_width, (c + 1) * o_width)
        for d in range(1, narrow):
            to_narrow(c, d).wait_recv()
        total = out_got[c, 0].astype(jnp.float32)
        for n in range(1, narrow):
            total = total + out_got[c, n].astype(jnp.float32)
        attn_out[:, cols] = total.astype(jnp.bfloat16)

    for block, (col, width) in enumerate(blocks):
        to_neighbour(block, col, width).wait_send()
        for d in range(1, pairs):
            to_owner(block, d, col, width).wait_send()
    for s in range(slots):
        for d in range(1, wide):
            to_wide(s, d).wait_send()
    for c in range(o_chunks):
        for d in range(1, narrow):
            to_narrow(c, d).wait_send()


def finish(attn, keys_new, values_new, attn_out, new_keys, new_values):
    attn_out[...] = attn[...]
    new_keys[...] = keys_new[...]
    new_values[...] = values_new[...]


def per_device(
    wide,
    narrow,
    hidden,
    w_query,
    w_key,
    w_value,
    w_out,
    key_cache,
    value_cache,
    cycle_offset,
    valid_length,
    slot_of,
):
    requests = slot_of.shape[0]
    slots, window, kv_local, head_dim = key_cache.shape
    query_cols = w_query.shape[1]
    key_cols = w_key.shape[1]
    out_cols = w_out.shape[1]
    q_width = width_of(query_cols, 512)
    o_width = width_of(out_cols, 512)
    q_chunks = query_cols // q_width
    o_chunks = out_cols // o_width
    all_cols = query_cols + 2 * key_cols
    span = window * kv_local
    vmem = pl.BlockSpec(memory_space=pltpu.VMEM)
    hbm = pl.BlockSpec(memory_space=pltpu.HBM)
    heads_local = query_cols // head_dim
    outs = (
        jax.ShapeDtypeStruct((requests, out_cols), jnp.bfloat16),
        jax.ShapeDtypeStruct((slots, key_cols), jnp.bfloat16),
        jax.ShapeDtypeStruct((slots, key_cols), jnp.bfloat16),
    )
    results = pl.pallas_call(
        functools.partial(kernel, wide, narrow, kv_local, q_width, o_width),
        out_shape=outs,
        in_specs=[hbm] * 10,
        out_specs=(vmem, vmem, vmem),
        scratch_shapes=[
            pltpu.VMEM(hidden.shape, jnp.bfloat16),
            pltpu.VMEM((1, requests), jnp.int32),
            pltpu.SMEM((slots,), jnp.int32),
            pltpu.SMEM((slots,), jnp.int32),
            pltpu.VMEM(w_query.shape, jnp.bfloat16),
            pltpu.VMEM(w_key.shape, jnp.bfloat16),
            pltpu.VMEM(w_value.shape, jnp.bfloat16),
            pltpu.VMEM(w_out.shape, jnp.bfloat16),
            pltpu.VMEM((slots, span, head_dim), jnp.bfloat16),
            pltpu.VMEM((slots, span, head_dim), jnp.bfloat16),
            pltpu.VMEM((2, wide // 2, slots, all_cols), jnp.float32),
            pltpu.VMEM((wide // 2, slots, all_cols), jnp.float32),
            pltpu.VMEM((wide // 2, slots, all_cols), jnp.float32),
            pltpu.VMEM((wide // 2, slots, all_cols), jnp.float32),
            pltpu.VMEM((slots, heads_local, head_dim), jnp.float32),
            pltpu.VMEM((slots, heads_local, head_dim), jnp.bfloat16),
            pltpu.VMEM((wide, slots, heads_local, head_dim), jnp.bfloat16),
            pltpu.VMEM((wide * slots, heads_local, head_dim), jnp.float32),
            pltpu.VMEM((o_chunks, requests, o_width), jnp.bfloat16),
            pltpu.VMEM((o_chunks, narrow, requests, o_width), jnp.bfloat16),
            pltpu.SemaphoreType.DMA((4 + q_chunks + o_chunks,)),
            pltpu.SemaphoreType.DMA((4,)),
            pltpu.SemaphoreType.DMA((1 + q_chunks,)),
            pltpu.SemaphoreType.DMA((1 + q_chunks,)),
            pltpu.SemaphoreType.DMA((1 + q_chunks, wide // 2)),
            pltpu.SemaphoreType.DMA((1 + q_chunks, wide // 2)),
            pltpu.SemaphoreType.DMA((slots, wide)),
            pltpu.SemaphoreType.DMA((slots, wide)),
            pltpu.SemaphoreType.DMA((o_chunks, narrow)),
            pltpu.SemaphoreType.DMA((o_chunks, narrow)),
        ],
        compiler_params=pltpu.CompilerParams(
            collective_id=0, has_side_effects=True, vmem_limit_bytes=63 * 1024 * 1024
        ),
        name="decode_step",
    )(
        hidden,
        w_query,
        w_key,
        w_value,
        w_out,
        key_cache.reshape(slots, span, head_dim),
        value_cache.reshape(slots, span, head_dim),
        slot_of.reshape(1, requests),
        cycle_offset,
        valid_length,
    )
    return pl.pallas_call(
        finish,
        out_shape=outs,
        in_specs=[vmem] * 3,
        out_specs=(vmem,) * 3,
        name="finish",
    )(*results)


def solution(mesh):
    placed = (
        P("groups", "wide"),
        P("wide", "narrow"),
        P("wide", "narrow"),
        P("wide", "narrow"),
        P("narrow", "wide"),
        P(("groups", "wide"), None, "narrow", None),
        P(("groups", "wide"), None, "narrow", None),
        P(("groups", "wide")),
        P(("groups", "wide")),
        P("groups"),
    )
    return jax.shard_map(
        functools.partial(per_device, mesh.shape["wide"], mesh.shape["narrow"]),
        mesh=mesh,
        in_specs=placed,
        out_specs=(
            P("groups", "wide"),
            P(("groups", "wide"), "narrow"),
            P(("groups", "wide"), "narrow"),
        ),
        check_vma=False,
    )
```

```python
import functools

import jax
import jax.numpy as jnp
from jax import lax
from jax.experimental import pallas as pl
from jax.experimental.pallas import tpu as pltpu
from jax.sharding import PartitionSpec as P

masked_low = -1e30
MESH = pl.DeviceIdType.MESH
q_most = 1024
o_most = 1024


def width_of(columns, most):
    width = min(columns, most)
    while columns % width:
        width -= 128
    return width


def kernel(
    wide,
    narrow,
    kv_local,
    q_width,
    o_width,
    hidden_in,
    w_query,
    w_key,
    w_value,
    w_out,
    key_cache,
    value_cache,
    slot_row_in,
    cycle_offset_in,
    valid_length_in,
    attn_out,
    new_keys,
    new_values,
    hidden,
    slot_row,
    cycle_offset,
    valid_length,
    wq,
    wk,
    wv,
    wo,
    keys,
    values,
    part,
    got,
    queries,
    heads_own,
    heads_got,
    heads_full,
    out_part,
    out_got,
    in_sem,
    small_sem,
    send_sem,
    recv_sem,
    head_send,
    head_recv,
    out_send,
    out_recv,
):
    me_wide = lax.axis_index("wide")
    me_narrow = lax.axis_index("narrow")
    requests = hidden.shape[0]
    slots = keys.shape[0]
    head_dim = keys.shape[2]
    span = keys.shape[1]
    window = span // kv_local
    query_cols = wq.shape[1]
    key_cols = wk.shape[1]
    out_cols = wo.shape[1]
    heads_local = query_cols // head_dim
    group = heads_local // kv_local
    q_chunks = query_cols // q_width
    o_chunks = out_cols // o_width

    first = [
        pltpu.make_async_copy(w_key, wk, in_sem.at[0]),
        pltpu.make_async_copy(w_value, wv, in_sem.at[1]),
    ]
    for c in range(q_chunks):
        cols = pl.ds(c * q_width, q_width)
        first.append(pltpu.make_async_copy(w_query.at[:, cols], wq.at[:, cols], in_sem.at[2 + c]))
    base = 2 + q_chunks
    cache_in = [
        pltpu.make_async_copy(key_cache, keys, in_sem.at[base]),
        pltpu.make_async_copy(value_cache, values, in_sem.at[base + 1]),
    ]
    out_in = []
    for c in range(o_chunks):
        cols = pl.ds(c * o_width, o_width)
        out_in.append(
            pltpu.make_async_copy(w_out.at[:, cols], wo.at[:, cols], in_sem.at[base + 2 + c])
        )
    small = [
        pltpu.make_async_copy(hidden_in, hidden, small_sem.at[0]),
        pltpu.make_async_copy(slot_row_in, slot_row, small_sem.at[1]),
        pltpu.make_async_copy(cycle_offset_in, cycle_offset, small_sem.at[2]),
        pltpu.make_async_copy(valid_length_in, valid_length, small_sem.at[3]),
    ]
    for copy in small + first:
        copy.start()

    barrier = pltpu.get_barrier_semaphore()
    peers = wide + narrow - 2
    for d in range(1, wide):
        pl.semaphore_signal(
            barrier,
            inc=1,
            device_id={"wide": lax.rem(me_wide + d, wide)},
            device_id_type=MESH,
        )
    for d in range(1, narrow):
        pl.semaphore_signal(
            barrier,
            inc=1,
            device_id={"narrow": lax.rem(me_narrow + d, narrow)},
            device_id_type=MESH,
        )

    small[0].wait()
    small[1].wait()
    slot_id = lax.broadcasted_iota(jnp.int32, (requests, requests), 0)
    pick = jnp.where(slot_row[...] == slot_id, 1.0, 0.0)
    rows = jnp.dot(
        pick.astype(jnp.bfloat16), hidden[...], preferred_element_type=jnp.float32
    ).astype(jnp.bfloat16)

    def to_owner(block, d):
        row, count = blocks[block]
        peer = lax.rem(me_wide + d, wide)
        return pltpu.make_async_remote_copy(
            src_ref=part.at[peer, pl.ds(row, count)],
            dst_ref=got.at[d, pl.ds(row, count)],
            send_sem=send_sem.at[block, d],
            recv_sem=recv_sem.at[block, d],
            device_id={"wide": peer},
            device_id_type=MESH,
        )

    key_rows = key_cols // head_dim * slots
    block_rows = q_width // head_dim * slots
    first_query = 2 * key_rows
    blocks = [(0, 2 * key_rows)] + [
        (first_query + c * block_rows, block_rows) for c in range(q_chunks)
    ]

    def keep(sums, row):
        for t in range(sums.shape[1] // head_dim):
            tile = sums[:, t * head_dim : (t + 1) * head_dim]
            for w in range(wide):
                part[w, row + t * slots : row + (t + 1) * slots] = tile[w * slots : (w + 1) * slots]

    for block, (row, count) in enumerate(blocks):
        if block == 0:
            first[0].wait()
            keep(jnp.dot(rows, wk[...], preferred_element_type=jnp.float32), 0)
            first[1].wait()
            keep(jnp.dot(rows, wv[...], preferred_element_type=jnp.float32), key_rows)
            pl.semaphore_wait(barrier, peers)
        else:
            first[1 + block].wait()
            cols = slice((block - 1) * q_width, block * q_width)
            keep(jnp.dot(rows, wq[:, cols], preferred_element_type=jnp.float32), row)
        for d in range(1, wide):
            to_owner(block, d).start()
    for copy in cache_in + out_in:
        copy.start()

    place = lax.broadcasted_iota(jnp.int32, (1, span), 1)
    position = place // kv_local
    kv_of = place - position * kv_local
    row_kv = lax.broadcasted_iota(jnp.int32, (heads_local, 1), 0) // group
    same_head = row_kv == kv_of
    scale = 1.0 / jnp.sqrt(jnp.float32(head_dim))

    def summed(block):
        row, count = blocks[block]
        total = part[me_wide, row : row + count]
        for d in range(1, wide):
            to_owner(block, d).wait_recv()
            total = total + got[d, row : row + count]
        return total

    fresh = summed(0).astype(jnp.bfloat16).astype(jnp.float32)
    keys_fresh = fresh[:key_rows]
    values_fresh = fresh[key_rows:]
    for k in range(kv_local):
        tile = slice(k * head_dim, (k + 1) * head_dim)
        new_keys[:, tile] = keys_fresh[k * slots : (k + 1) * slots].astype(jnp.bfloat16)
        new_values[:, tile] = values_fresh[k * slots : (k + 1) * slots].astype(jnp.bfloat16)
    for block in range(1, len(blocks)):
        row, count = blocks[block]
        queries[row - first_query : row - first_query + count] = summed(block)

    for copy in cache_in + small[2:]:
        copy.wait()

    def by_head(fresh, s):
        result = jnp.broadcast_to(fresh[s : s + 1], (heads_local, head_dim))
        for k in range(1, kv_local):
            other = fresh[k * slots + s : k * slots + s + 1]
            result = jnp.where(row_kv == k, other, result)
        return result

    def to_wide(d):
        return pltpu.make_async_remote_copy(
            src_ref=heads_own,
            dst_ref=heads_got.at[d],
            send_sem=head_send.at[d],
            recv_sem=head_recv.at[d],
            device_id={"wide": lax.rem(me_wide + d, wide)},
            device_id_type=MESH,
        )

    for s in range(slots):
        query = queries[pl.ds(s, heads_local, stride=slots), :].astype(jnp.bfloat16)
        scores = (
            lax.dot_general(
                query, keys[s], (((1,), (1,)), ((), ())), preferred_element_type=jnp.float32
            )
            * scale
        )
        own_score = (
            jnp.sum(query.astype(jnp.float32) * by_head(keys_fresh, s), axis=1, keepdims=True)
            * scale
        )
        offset = cycle_offset[s]
        distance = offset - position
        distance = jnp.where(distance < 0, distance + window, distance)
        usable = (distance > 0) & (distance < valid_length[s])
        masked = jnp.where(usable & same_head, scores, masked_low)
        top = jnp.maximum(jnp.max(masked, axis=1, keepdims=True), own_score)
        spread = jnp.exp(masked - top)
        own = jnp.exp(own_score - top)
        inverse = 1.0 / (jnp.sum(spread, axis=1, keepdims=True) + own)
        mixed = jnp.dot(
            (spread * inverse).astype(jnp.bfloat16), values[s], preferred_element_type=jnp.float32
        )
        own_weight = (own * inverse).astype(jnp.bfloat16).astype(jnp.float32)
        heads_own[s] = (mixed + own_weight * by_head(values_fresh, s)).astype(jnp.bfloat16)
    for d in range(1, wide):
        to_wide(d).start()

    heads_full[0:slots] = heads_own[...].astype(jnp.float32)
    for d in range(1, wide):
        to_wide(d).wait_recv()
        heads_full[d * slots : (d + 1) * slots] = heads_got[d].astype(jnp.float32)
    held_row = lax.broadcasted_iota(jnp.int32, (requests, requests), 0)
    back = held_row // slots
    held_slot = lax.rem(me_wide - back + wide, wide) * slots + (held_row - back * slots)
    give = jnp.where(slot_row[...] == held_slot, 1.0, 0.0).astype(jnp.bfloat16)
    by_slot = jnp.concatenate(
        [heads_full[:, h, :].astype(jnp.bfloat16) for h in range(heads_local)], axis=1
    )
    heads = lax.dot_general(
        give,
        by_slot,
        (((0,), (0,)), ((), ())),
        preferred_element_type=jnp.float32,
    ).astype(jnp.bfloat16)

    def to_narrow(c, d):
        return pltpu.make_async_remote_copy(
            src_ref=out_part.at[c],
            dst_ref=out_got.at[c, me_narrow],
            send_sem=out_send.at[c, d],
            recv_sem=out_recv.at[c, d],
            device_id={"narrow": lax.rem(me_narrow + d, narrow)},
            device_id_type=MESH,
        )

    for c in range(o_chunks):
        cols = slice(c * o_width, (c + 1) * o_width)
        out_in[c].wait()
        sums = jnp.dot(heads, wo[:, cols], preferred_element_type=jnp.float32)
        out_part[c] = sums.astype(jnp.bfloat16)
        for d in range(1, narrow):
            to_narrow(c, d).start()
        out_got[c, me_narrow] = sums.astype(jnp.bfloat16)
    for c in range(o_chunks):
        cols = slice(c * o_width, (c + 1) * o_width)
        for d in range(1, narrow):
            to_narrow(c, d).wait_recv()
        total = out_got[c, 0].astype(jnp.float32)
        for n in range(1, narrow):
            total = total + out_got[c, n].astype(jnp.float32)
        attn_out[:, cols] = total.astype(jnp.bfloat16)

    for block in range(len(blocks)):
        for d in range(1, wide):
            to_owner(block, d).wait_send()
    for d in range(1, wide):
        to_wide(d).wait_send()
    for c in range(o_chunks):
        for d in range(1, narrow):
            to_narrow(c, d).wait_send()


def finish(attn, keys_new, values_new, attn_out, new_keys, new_values):
    attn_out[...] = attn[...]
    new_keys[...] = keys_new[...]
    new_values[...] = values_new[...]


def per_device(
    wide,
    narrow,
    hidden,
    w_query,
    w_key,
    w_value,
    w_out,
    key_cache,
    value_cache,
    cycle_offset,
    valid_length,
    slot_of,
):
    requests = slot_of.shape[0]
    slots, window, kv_local, head_dim = key_cache.shape
    query_cols = w_query.shape[1]
    key_cols = w_key.shape[1]
    out_cols = w_out.shape[1]
    q_width = width_of(query_cols, q_most)
    o_width = width_of(out_cols, o_most)
    q_chunks = query_cols // q_width
    o_chunks = out_cols // o_width
    all_rows = (query_cols + 2 * key_cols) // head_dim * slots
    span = window * kv_local
    vmem = pl.BlockSpec(memory_space=pltpu.VMEM)
    hbm = pl.BlockSpec(memory_space=pltpu.HBM)
    heads_local = query_cols // head_dim
    outs = (
        jax.ShapeDtypeStruct((requests, out_cols), jnp.bfloat16),
        jax.ShapeDtypeStruct((slots, key_cols), jnp.bfloat16),
        jax.ShapeDtypeStruct((slots, key_cols), jnp.bfloat16),
    )
    results = pl.pallas_call(
        functools.partial(kernel, wide, narrow, kv_local, q_width, o_width),
        out_shape=outs,
        in_specs=[hbm] * 10,
        out_specs=(vmem, vmem, vmem),
        scratch_shapes=[
            pltpu.VMEM(hidden.shape, jnp.bfloat16),
            pltpu.VMEM((1, requests), jnp.int32),
            pltpu.SMEM((slots,), jnp.int32),
            pltpu.SMEM((slots,), jnp.int32),
            pltpu.VMEM(w_query.shape, jnp.bfloat16),
            pltpu.VMEM(w_key.shape, jnp.bfloat16),
            pltpu.VMEM(w_value.shape, jnp.bfloat16),
            pltpu.VMEM(w_out.shape, jnp.bfloat16),
            pltpu.VMEM((slots, span, head_dim), jnp.bfloat16),
            pltpu.VMEM((slots, span, head_dim), jnp.bfloat16),
            pltpu.VMEM((wide, all_rows, head_dim), jnp.float32),
            pltpu.VMEM((wide, all_rows, head_dim), jnp.float32),
            pltpu.VMEM((heads_local * slots, head_dim), jnp.float32),
            pltpu.VMEM((slots, heads_local, head_dim), jnp.bfloat16),
            pltpu.VMEM((wide, slots, heads_local, head_dim), jnp.bfloat16),
            pltpu.VMEM((wide * slots, heads_local, head_dim), jnp.float32),
            pltpu.VMEM((o_chunks, requests, o_width), jnp.bfloat16),
            pltpu.VMEM((o_chunks, narrow, requests, o_width), jnp.bfloat16),
            pltpu.SemaphoreType.DMA((4 + q_chunks + o_chunks,)),
            pltpu.SemaphoreType.DMA((4,)),
            pltpu.SemaphoreType.DMA((1 + q_chunks, wide)),
            pltpu.SemaphoreType.DMA((1 + q_chunks, wide)),
            pltpu.SemaphoreType.DMA((wide,)),
            pltpu.SemaphoreType.DMA((wide,)),
            pltpu.SemaphoreType.DMA((o_chunks, narrow)),
            pltpu.SemaphoreType.DMA((o_chunks, narrow)),
        ],
        compiler_params=pltpu.CompilerParams(
            collective_id=0, has_side_effects=True, vmem_limit_bytes=63 * 1024 * 1024
        ),
        name="decode_step",
    )(
        hidden,
        w_query,
        w_key,
        w_value,
        w_out,
        key_cache.reshape(slots, span, head_dim),
        value_cache.reshape(slots, span, head_dim),
        slot_of.reshape(1, requests),
        cycle_offset,
        valid_length,
    )
    return pl.pallas_call(
        finish,
        out_shape=outs,
        in_specs=[vmem] * 3,
        out_specs=(vmem,) * 3,
        name="finish",
    )(*results)


def solution(mesh):
    placed = (
        P("groups", "wide"),
        P("wide", "narrow"),
        P("wide", "narrow"),
        P("wide", "narrow"),
        P("narrow", "wide"),
        P(("groups", "wide"), None, "narrow", None),
        P(("groups", "wide"), None, "narrow", None),
        P(("groups", "wide")),
        P(("groups", "wide")),
        P("groups"),
    )
    return jax.shard_map(
        functools.partial(per_device, mesh.shape["wide"], mesh.shape["narrow"]),
        mesh=mesh,
        in_specs=placed,
        out_specs=(
            P("groups", "wide"),
            P(("groups", "wide"), "narrow"),
            P(("groups", "wide"), "narrow"),
        ),
        check_vma=False,
    )
```

```python
import functools

import jax
import jax.numpy as jnp
from jax import lax
from jax.experimental import pallas as pl
from jax.experimental.pallas import tpu as pltpu
from jax.sharding import PartitionSpec as P

masked_low = -1e30
MESH = pl.DeviceIdType.MESH
q_parts = (4, 4)
finish_kib = 1024
main_kib = 64512
far = False
o_most = 1024


def width_of(columns, most):
    width = min(columns, most)
    while columns % width:
        width -= 128
    return width


def blocks_of(columns, parts):
    result, col, done = [], 0, 0
    for share in parts:
        done += share
        end = columns // 128 * done // sum(parts) * 128
        if end > col:
            result.append((col, end - col))
        col = end
    return tuple(result)


def kernel(
    wide,
    narrow,
    kv_local,
    q_blocks,
    o_width,
    hidden_in,
    w_query,
    w_key,
    w_value,
    w_out,
    key_cache,
    value_cache,
    slot_row_in,
    cycle_offset_in,
    valid_length_in,
    attn_out,
    new_keys,
    new_values,
    hidden,
    slot_row,
    cycle_offset,
    valid_length,
    wq,
    wk,
    wv,
    wo,
    keys,
    values,
    part,
    got,
    queries,
    allowed,
    heads_own,
    heads_got,
    heads_full,
    out_part,
    out_got,
    in_sem,
    small_sem,
    send_sem,
    recv_sem,
    head_send,
    head_recv,
    out_send,
    out_recv,
):
    me_wide = lax.axis_index("wide")
    me_narrow = lax.axis_index("narrow")
    requests = hidden.shape[0]
    slots = keys.shape[0]
    head_dim = keys.shape[2]
    span = keys.shape[1]
    window = span // kv_local
    query_cols = wq.shape[1]
    key_cols = wk.shape[1]
    out_cols = wo.shape[1]
    heads_local = query_cols // head_dim
    group = heads_local // kv_local
    q_chunks = len(q_blocks)
    o_chunks = out_cols // o_width

    first = [
        pltpu.make_async_copy(w_key, wk, in_sem.at[0]),
        pltpu.make_async_copy(w_value, wv, in_sem.at[1]),
    ]
    for c, (col, width) in enumerate(q_blocks):
        cols = pl.ds(col, width)
        first.append(pltpu.make_async_copy(w_query.at[:, cols], wq.at[:, cols], in_sem.at[2 + c]))
    base = 2 + q_chunks
    cache_in = [
        pltpu.make_async_copy(key_cache, keys, in_sem.at[base]),
        pltpu.make_async_copy(value_cache, values, in_sem.at[base + 1]),
    ]
    out_in = []
    for c in range(o_chunks):
        cols = pl.ds(c * o_width, o_width)
        out_in.append(
            pltpu.make_async_copy(w_out.at[:, cols], wo.at[:, cols], in_sem.at[base + 2 + c])
        )
    small = [
        pltpu.make_async_copy(hidden_in, hidden, small_sem.at[0]),
        pltpu.make_async_copy(slot_row_in, slot_row, small_sem.at[1]),
        pltpu.make_async_copy(cycle_offset_in, cycle_offset, small_sem.at[2]),
        pltpu.make_async_copy(valid_length_in, valid_length, small_sem.at[3]),
    ]
    for copy in small + first:
        copy.start()

    barrier = pltpu.get_barrier_semaphore()
    peers = wide + narrow - 2
    for d in range(1, wide):
        pl.semaphore_signal(
            barrier,
            inc=1,
            device_id={"wide": lax.rem(me_wide + d, wide)},
            device_id_type=MESH,
        )
    for d in range(1, narrow):
        pl.semaphore_signal(
            barrier,
            inc=1,
            device_id={"narrow": lax.rem(me_narrow + d, narrow)},
            device_id_type=MESH,
        )

    small[0].wait()
    small[1].wait()
    slot_id = lax.broadcasted_iota(jnp.int32, (requests, requests), 0)
    pick = jnp.where(slot_row[...] == slot_id, 1.0, 0.0)
    rows = jnp.dot(
        pick.astype(jnp.bfloat16), hidden[...], preferred_element_type=jnp.float32
    ).astype(jnp.bfloat16)

    def to_owner(block, d):
        row, count = blocks[block]
        peer = lax.rem(me_wide + d, wide)
        return pltpu.make_async_remote_copy(
            src_ref=part.at[peer, pl.ds(row, count)],
            dst_ref=got.at[d, pl.ds(row, count)],
            send_sem=send_sem.at[block, d],
            recv_sem=recv_sem.at[block, d],
            device_id={"wide": peer},
            device_id_type=MESH,
        )

    key_rows = key_cols // head_dim * slots
    first_query = 2 * key_rows
    blocks = [(0, 2 * key_rows)] + [
        (first_query + col // head_dim * slots, width // head_dim * slots)
        for col, width in q_blocks
    ]

    def keep(sums, row):
        for t in range(sums.shape[1] // head_dim):
            tile = sums[:, t * head_dim : (t + 1) * head_dim]
            for w in range(wide):
                part[w, row + t * slots : row + (t + 1) * slots] = tile[w * slots : (w + 1) * slots]

    for block, (row, count) in enumerate(blocks):
        if block == 0:
            first[0].wait()
            keep(jnp.dot(rows, wk[...], preferred_element_type=jnp.float32), 0)
            first[1].wait()
            keep(jnp.dot(rows, wv[...], preferred_element_type=jnp.float32), key_rows)
            pl.semaphore_wait(barrier, peers)
        else:
            first[1 + block].wait()
            col, width = q_blocks[block - 1]
            keep(jnp.dot(rows, wq[:, col : col + width], preferred_element_type=jnp.float32), row)
        for d in range(wide - 1, 0, -1) if far else range(1, wide):
            to_owner(block, d).start()
    for copy in cache_in + out_in:
        copy.start()

    place = lax.broadcasted_iota(jnp.int32, (1, span), 1)
    position = place // kv_local
    kv_of = place - position * kv_local
    row_kv = lax.broadcasted_iota(jnp.int32, (heads_local, 1), 0) // group
    same_head = row_kv == kv_of
    scale = 1.0 / jnp.sqrt(jnp.float32(head_dim))

    for copy in small[2:]:
        copy.wait()
    for s in range(slots):
        distance = cycle_offset[s] - position
        distance = jnp.where(distance < 0, distance + window, distance)
        usable = (distance > 0) & (distance < valid_length[s])
        allowed[s] = jnp.where(usable & same_head, 1.0, 0.0)

    def summed(block):
        row, count = blocks[block]
        total = part[me_wide, row : row + count]
        for d in range(1, wide):
            to_owner(block, d).wait_recv()
            total = total + got[d, row : row + count]
        return total

    fresh = summed(0).astype(jnp.bfloat16).astype(jnp.float32)
    keys_fresh = fresh[:key_rows]
    values_fresh = fresh[key_rows:]
    for k in range(kv_local):
        tile = slice(k * head_dim, (k + 1) * head_dim)
        new_keys[:, tile] = keys_fresh[k * slots : (k + 1) * slots].astype(jnp.bfloat16)
        new_values[:, tile] = values_fresh[k * slots : (k + 1) * slots].astype(jnp.bfloat16)
    for block in range(1, len(blocks)):
        row, count = blocks[block]
        queries[row - first_query : row - first_query + count] = summed(block)

    for copy in cache_in:
        copy.wait()

    def by_head(fresh, s):
        result = jnp.broadcast_to(fresh[s : s + 1], (heads_local, head_dim))
        for k in range(1, kv_local):
            other = fresh[k * slots + s : k * slots + s + 1]
            result = jnp.where(row_kv == k, other, result)
        return result

    def to_wide(d):
        return pltpu.make_async_remote_copy(
            src_ref=heads_own,
            dst_ref=heads_got.at[d],
            send_sem=head_send.at[d],
            recv_sem=head_recv.at[d],
            device_id={"wide": lax.rem(me_wide + d, wide)},
            device_id_type=MESH,
        )

    query, scores = [], []
    for s in range(slots):
        query.append(queries[pl.ds(s, heads_local, stride=slots), :].astype(jnp.bfloat16))
        scores.append(
            lax.dot_general(
                query[s], keys[s], (((1,), (1,)), ((), ())), preferred_element_type=jnp.float32
            )
            * scale
        )
    weights, own_weight = [], []
    for s in range(slots):
        own_score = (
            jnp.sum(query[s].astype(jnp.float32) * by_head(keys_fresh, s), axis=1, keepdims=True)
            * scale
        )
        masked = jnp.where(allowed[s] > 0.0, scores[s], masked_low)
        top = jnp.maximum(jnp.max(masked, axis=1, keepdims=True), own_score)
        spread = jnp.exp(masked - top)
        own = jnp.exp(own_score - top)
        inverse = 1.0 / (jnp.sum(spread, axis=1, keepdims=True) + own)
        weights.append((spread * inverse).astype(jnp.bfloat16))
        own_weight.append((own * inverse).astype(jnp.bfloat16).astype(jnp.float32))
    for s in range(slots):
        mixed = jnp.dot(weights[s], values[s], preferred_element_type=jnp.float32)
        heads_own[s] = (mixed + own_weight[s] * by_head(values_fresh, s)).astype(jnp.bfloat16)
    for d in range(1, wide):
        to_wide(d).start()

    heads_full[0:slots] = heads_own[...].astype(jnp.float32)
    for d in range(1, wide):
        to_wide(d).wait_recv()
        heads_full[d * slots : (d + 1) * slots] = heads_got[d].astype(jnp.float32)
    held_row = lax.broadcasted_iota(jnp.int32, (requests, requests), 0)
    back = held_row // slots
    held_slot = lax.rem(me_wide - back + wide, wide) * slots + (held_row - back * slots)
    give = jnp.where(slot_row[...] == held_slot, 1.0, 0.0).astype(jnp.bfloat16)
    by_slot = jnp.concatenate(
        [heads_full[:, h, :].astype(jnp.bfloat16) for h in range(heads_local)], axis=1
    )
    heads = lax.dot_general(
        give,
        by_slot,
        (((0,), (0,)), ((), ())),
        preferred_element_type=jnp.float32,
    ).astype(jnp.bfloat16)

    def to_narrow(c, d):
        return pltpu.make_async_remote_copy(
            src_ref=out_part.at[c],
            dst_ref=out_got.at[c, me_narrow],
            send_sem=out_send.at[c, d],
            recv_sem=out_recv.at[c, d],
            device_id={"narrow": lax.rem(me_narrow + d, narrow)},
            device_id_type=MESH,
        )

    for c in range(o_chunks):
        cols = slice(c * o_width, (c + 1) * o_width)
        out_in[c].wait()
        sums = jnp.dot(heads, wo[:, cols], preferred_element_type=jnp.float32)
        out_part[c] = sums.astype(jnp.bfloat16)
        for d in range(1, narrow):
            to_narrow(c, d).start()
        out_got[c, me_narrow] = sums.astype(jnp.bfloat16)
    for c in range(o_chunks):
        cols = slice(c * o_width, (c + 1) * o_width)
        for d in range(1, narrow):
            to_narrow(c, d).wait_recv()
        total = out_got[c, 0].astype(jnp.float32)
        for n in range(1, narrow):
            total = total + out_got[c, n].astype(jnp.float32)
        attn_out[:, cols] = total.astype(jnp.bfloat16)

    for block in range(len(blocks)):
        for d in range(1, wide):
            to_owner(block, d).wait_send()
    for d in range(1, wide):
        to_wide(d).wait_send()
    for c in range(o_chunks):
        for d in range(1, narrow):
            to_narrow(c, d).wait_send()


def finish(attn, keys_new, values_new, attn_out, new_keys, new_values):
    attn_out[...] = attn[...]
    new_keys[...] = keys_new[...]
    new_values[...] = values_new[...]


def per_device(
    wide,
    narrow,
    hidden,
    w_query,
    w_key,
    w_value,
    w_out,
    key_cache,
    value_cache,
    cycle_offset,
    valid_length,
    slot_of,
):
    requests = slot_of.shape[0]
    slots, window, kv_local, head_dim = key_cache.shape
    query_cols = w_query.shape[1]
    key_cols = w_key.shape[1]
    out_cols = w_out.shape[1]
    q_blocks = blocks_of(query_cols, q_parts)
    o_width = width_of(out_cols, o_most)
    q_chunks = len(q_blocks)
    o_chunks = out_cols // o_width
    all_rows = (query_cols + 2 * key_cols) // head_dim * slots
    span = window * kv_local
    vmem = pl.BlockSpec(memory_space=pltpu.VMEM)
    hbm = pl.BlockSpec(memory_space=pltpu.HBM)
    heads_local = query_cols // head_dim
    outs = (
        jax.ShapeDtypeStruct((requests, out_cols), jnp.bfloat16),
        jax.ShapeDtypeStruct((slots, key_cols), jnp.bfloat16),
        jax.ShapeDtypeStruct((slots, key_cols), jnp.bfloat16),
    )
    results = pl.pallas_call(
        functools.partial(kernel, wide, narrow, kv_local, q_blocks, o_width),
        out_shape=tuple(pltpu.VMEM(out.shape, out.dtype) for out in outs),
        in_specs=[hbm] * 10,
        out_specs=(vmem, vmem, vmem),
        scratch_shapes=[
            pltpu.VMEM(hidden.shape, jnp.bfloat16),
            pltpu.VMEM((1, requests), jnp.int32),
            pltpu.SMEM((slots,), jnp.int32),
            pltpu.SMEM((slots,), jnp.int32),
            pltpu.VMEM(w_query.shape, jnp.bfloat16),
            pltpu.VMEM(w_key.shape, jnp.bfloat16),
            pltpu.VMEM(w_value.shape, jnp.bfloat16),
            pltpu.VMEM(w_out.shape, jnp.bfloat16),
            pltpu.VMEM((slots, span, head_dim), jnp.bfloat16),
            pltpu.VMEM((slots, span, head_dim), jnp.bfloat16),
            pltpu.VMEM((wide, all_rows, head_dim), jnp.float32),
            pltpu.VMEM((wide, all_rows, head_dim), jnp.float32),
            pltpu.VMEM((heads_local * slots, head_dim), jnp.float32),
            pltpu.VMEM((slots, heads_local, span), jnp.float32),
            pltpu.VMEM((slots, heads_local, head_dim), jnp.bfloat16),
            pltpu.VMEM((wide, slots, heads_local, head_dim), jnp.bfloat16),
            pltpu.VMEM((wide * slots, heads_local, head_dim), jnp.float32),
            pltpu.VMEM((o_chunks, requests, o_width), jnp.bfloat16),
            pltpu.VMEM((o_chunks, narrow, requests, o_width), jnp.bfloat16),
            pltpu.SemaphoreType.DMA((4 + q_chunks + o_chunks,)),
            pltpu.SemaphoreType.DMA((4,)),
            pltpu.SemaphoreType.DMA((1 + q_chunks, wide)),
            pltpu.SemaphoreType.DMA((1 + q_chunks, wide)),
            pltpu.SemaphoreType.DMA((wide,)),
            pltpu.SemaphoreType.DMA((wide,)),
            pltpu.SemaphoreType.DMA((o_chunks, narrow)),
            pltpu.SemaphoreType.DMA((o_chunks, narrow)),
        ],
        compiler_params=pltpu.CompilerParams(
            collective_id=0, has_side_effects=True, vmem_limit_bytes=main_kib * 1024
        ),
        name="decode_step",
    )(
        hidden,
        w_query,
        w_key,
        w_value,
        w_out,
        key_cache.reshape(slots, span, head_dim),
        value_cache.reshape(slots, span, head_dim),
        slot_of.reshape(1, requests),
        cycle_offset,
        valid_length,
    )
    return pl.pallas_call(
        finish,
        out_shape=outs,
        in_specs=[vmem] * 3,
        out_specs=(vmem,) * 3,
        compiler_params=pltpu.CompilerParams(vmem_limit_bytes=finish_kib * 1024),
        name="finish",
    )(*results)


def solution(mesh):
    placed = (
        P("groups", "wide"),
        P("wide", "narrow"),
        P("wide", "narrow"),
        P("wide", "narrow"),
        P("narrow", "wide"),
        P(("groups", "wide"), None, "narrow", None),
        P(("groups", "wide"), None, "narrow", None),
        P(("groups", "wide")),
        P(("groups", "wide")),
        P("groups"),
    )
    return jax.shard_map(
        functools.partial(per_device, mesh.shape["wide"], mesh.shape["narrow"]),
        mesh=mesh,
        in_specs=placed,
        out_specs=(
            P("groups", "wide"),
            P(("groups", "wide"), "narrow"),
            P(("groups", "wide"), "narrow"),
        ),
        check_vma=False,
    )
```
